512 devices in a mesh: scalp: 256 (over z, y, x), screen: 2 (over core).
Axes of the slice: x: 4, y: 8, z: 8, core: 2. Of those that a mesh axis runs over, the one named last changes fastest.
Arguments:
- guides: bfloat16 [1048576, 384], P('scalp'), may hold values from -6 to 6
- neighbours: int32 [2048, 32], P(('scalp', 'screen')), may hold values from 0 to 1048575, as said below
- pick: int32 [2048, 4, 256], P(('scalp', 'screen')), may hold values from 0 to 31, as said below
- pick_weight: bfloat16 [2048, 4, 256], P(('scalp', 'screen')), may hold values from 0.099609375 to 0.59765625
- keep: int32 [2048, 256], P(('scalp', 'screen')), may hold values 0 or 1
- width: float32 [2048, 256], P(('scalp', 'screen')), may hold values from 0.2 to 2
- route: int32 [2048, 1], P(('scalp', 'screen')), may hold values from 0 to 1; in each aligned block of 4 rows (0 to 3, 4 to 7, ...) at most 3 rows name the same one
- tess_centre: bfloat16 [2, 384, 768], P('screen'), may hold values from -0.3125 to 0.3125
- tess_side: bfloat16 [2, 384, 768], P('screen'), may hold values from -0.3125 to 0.3125
Outputs:
- ribbon: bfloat16 [786432, 768], P(('scalp', 'screen'))
The draws below stay inside these ranges and needn't reach their ends.
Inputs may be any that keep to these rules, and one draw needn't show every extreme that they name: `neighbours`: each entry names a guide of the render block's own scalp tile or of the scalp tile just before or after it, wrapping around; a block of device (s, c) belongs to scalp tile s. `pick`: the 4 entries of one render strand differ. `route`: among the 4 blocks of one device at most 3 name the same screen tile.
All inputs are finite; a program needn't handle non-finite values. No bound on the sum of `keep` on one device may be relied on, other than what follows from the above.
Results may differ from the reference program's by a relative error of at most 0.009.
Values may be sent and summed in bfloat16 or wider, within the bound.
No kernel may reach another device: no remote copies, remote signals or barrier semaphores. Data moves between devices by JAX's collectives and lax.ppermute only.
A program may use at most 64 MiB of HBM per device.

```python
import math
import jax
import jax.numpy as jnp
import numpy as np
from jax import lax

P_SIZE = 128
BLK = 256
K = 32
J = 4
RB = 4
GT = 4096
TILES = 256
SCREENS = 2
CAP = 3
GUIDES = 1048576
RBLOCKS = 2048


def draw_neighbours(key, part):
    first, second = jax.random.split(key)
    block = jnp.arange(RBLOCKS, dtype=jnp.int32)
    home = block // (RB * SCREENS)
    offset = jax.random.randint(first, (RBLOCKS, K), -1, 2).astype(jnp.int32)
    within = jax.random.randint(second, (RBLOCKS, K), 0, GT).astype(jnp.int32)
    offset = offset.at[0, 0].set(0).at[RBLOCKS - 1, K - 1].set(0)
    within = within.at[0, 0].set(0).at[RBLOCKS - 1, K - 1].set(GT - 1)
    return ((home[:, None] + offset) % TILES * GT + within).astype(jnp.int32)


def draw_pick(key, part):
    scores = jax.random.randint(key, (RBLOCKS, BLK, K), 0, 1 << 20).astype(jnp.int32) * K + jnp.arange(K, dtype=jnp.int32)
    order = jnp.argsort(scores, axis=-1)[..., :J]
    return jnp.transpose(order, (0, 2, 1)).astype(jnp.int32)


def set_ends(drawn, key, least, high):
    index_at = [jax.random.randint(jax.random.fold_in(key, axis), (), 0, length) for axis, length in enumerate(drawn.shape)]
    widest = drawn.shape.index(max(drawn.shape))
    beside = index_at[:widest] + [(index_at[widest] + 1) % drawn.shape[widest]] + index_at[widest + 1:]
    return drawn.at[tuple(index_at)].set(least).at[tuple(beside)].set(high)


def block_scale(own_key, extent, shards, low, largest):
    loudness, own = 1.0, jax.random.fold_in(own_key, 6)
    for dim, blocks in shards:
        heights = jnp.exp(jax.random.uniform(jax.random.fold_in(own, dim), (blocks,), jnp.float32, low / len(shards), largest / len(shards)))
        loudness = loudness * jnp.repeat(heights, extent[dim] // blocks).reshape([-1 if axis == dim else 1 for axis in range(len(extent))])
    return loudness


def shared_out(rng, own, number, rows, amount, top, most, slope):
    ranking = jax.random.permutation(rng, amount)
    heavy_load, usual = shares(amount, rows * top, most, slope, True), shares(amount, rows * top, most, slope, False)
    places = jnp.arange(amount)

    def named(tallies, turn):
        used = int((tallies > 0).sum())
        fixed = max(1, used // 4)
        passed = fixed + (places - fixed + turn * (used - fixed)) % max(1, amount - fixed)
        return jnp.zeros((amount,), jnp.int32).at[ranking[jnp.where(places < fixed, places, passed)]].set(jnp.asarray(tallies, jnp.int32))

    tallies = jnp.where(number % 4 == 0, named(heavy_load, number // 4), named(usual, number - number // 4 - 1))
    mixed = jax.random.permutation(jax.random.fold_in(own, 3), amount)
    source_of, taker = mixed[0:amount // 2 * 2:2], mixed[1:amount // 2 * 2:2]
    margin = jnp.minimum(tallies[source_of] - 1, most - tallies[taker]) // 2
    margin = jnp.where((source_of == ranking[0]) | (taker == ranking[0]) | (tallies[taker] == 0), 0, jnp.maximum(margin, 0))
    passed = jax.random.randint(jax.random.fold_in(own, 4), (amount // 2,), 0, 1 << 20) % (margin + 1)
    tallies = tallies.at[source_of].add(-passed).at[taker].add(passed)
    members = jnp.searchsorted(jnp.cumsum(tallies), jnp.arange(rows * top), side="right").astype(jnp.int32)
    table = members.reshape(top, rows).T
    table = table[jax.random.permutation(jax.random.fold_in(own, 1), rows)]
    turn = jax.random.randint(jax.random.fold_in(own, 2), (rows, 1), 0, top)
    return jnp.take_along_axis(table, (jnp.arange(top)[None, :] + turn) % top, axis=1)


def shares(count, total, reach, lean, full):
    weights = [(1 << 20) // math.isqrt(rank ** lean) + 1 for rank in range(1, count + 1)]
    largest = reach if full else min(reach, max(-(-total // count), total * weights[0] // sum(weights)))
    least = 1 if total - largest >= count - 1 else 0
    holding, rest = [largest] + [least] * (count - 1), total - largest - least * (count - 1)
    while rest > 0:
        free = [i for i in range(1, count) if holding[i] < largest] or [i for i in range(1, count) if holding[i] < reach]
        pool, left = sum([weights[i] for i in free]), rest
        for i in free:
            addition = min(reach - holding[i], max(1, left * weights[i] // pool), rest)
            holding[i] = holding[i] + addition
            rest = rest - addition
    return np.array(holding)


def centred(rng, extent, spread, reach, cuts=(), held_as=jnp.bfloat16):
    result = spread * jax.random.normal(rng, extent, jnp.float32)
    if cuts:
        result = result * block_scale(rng, extent, cuts, -0.22, 0.18)
    return jnp.clip(result, -reach, reach).astype(held_as)


def setup_inputs(seed: int = 0) -> dict:
    splits = jax.random.split(jax.random.key(seed), 10)
    guides = centred(splits[0], (GUIDES, 3 * P_SIZE), 1.0, 6.0, ((0, 256),))
    neighbours = draw_neighbours(jax.random.fold_in(splits[9], 71), 0)
    pick = draw_pick(jax.random.fold_in(splits[9], 71), 0)
    pick_weight = jnp.clip(0.099609375 + 0.49804688 * jax.random.uniform(splits[3], (RBLOCKS, J, BLK), jnp.float32) ** block_scale(splits[3], (RBLOCKS, J, BLK), ((0, 512),), -0.2, 0.2), 0.099609375, 0.59765625).astype(jnp.bfloat16)
    keep = set_ends((jax.random.randint(splits[4], (RBLOCKS, BLK), 0, 4) < 3).astype(jnp.int32), jax.random.fold_in(splits[4], 1), 0, 1)
    width = jnp.clip(jnp.exp(math.log(2.0) - 2.3025851 * jax.random.uniform(splits[5], (RBLOCKS, BLK), jnp.float32) ** block_scale(splits[5], (RBLOCKS, BLK), ((0, 512),), -0.2, 0.2)), 0.2, 2.0)
    route_keys = jax.random.split(jax.random.fold_in(splits[6], 1), RBLOCKS // RB)
    route_turns = jax.random.permutation(jax.random.fold_in(splits[6], 3), RBLOCKS // RB)
    route = jax.vmap(lambda own, number: shared_out(jax.random.fold_in(splits[6], 2), own, number, RB, SCREENS, 1, CAP, 2))(route_keys, route_turns).reshape((RBLOCKS, 1))
    tess_centre = centred(splits[7], (SCREENS, 3 * P_SIZE, 6 * P_SIZE), (3 * P_SIZE) ** -0.5, 0.3125, ((0, 2),))
    tess_side = centred(splits[8], (SCREENS, 3 * P_SIZE, 6 * P_SIZE), (3 * P_SIZE) ** -0.5, 0.3125, ((0, 2),))
    return {"guides": guides, "neighbours": neighbours, "pick": pick, "pick_weight": pick_weight, "keep": keep, "width": width, "route": route, "tess_centre": tess_centre, "tess_side": tess_side}


def blend(picks, weights):
    hit = (picks[..., None] == jnp.arange(K, dtype=jnp.int32)).astype(jnp.float32)
    return jnp.sum(hit * weights.astype(jnp.float32)[..., None], axis=1).astype(jnp.bfloat16)


def reference(guides, neighbours, pick, pick_weight, keep, width, route, tess_centre, tess_side):
    ndev = TILES * SCREENS
    cap = RB // SCREENS + RB // 4

    def one_device(device):
        start = (device * RB).astype(jnp.int32)
        near = lax.dynamic_slice_in_dim(neighbours, start, RB, 0)
        picks = lax.dynamic_slice_in_dim(pick, start, RB, 0)
        weights = lax.dynamic_slice_in_dim(pick_weight, start, RB, 0)
        kept = lax.dynamic_slice_in_dim(keep, start, RB, 0).astype(jnp.float32)
        widths = lax.dynamic_slice_in_dim(width, start, RB, 0)
        tiles = lax.dynamic_slice_in_dim(route, start, RB, 0)[:, 0]
        gathered = guides[near]
        mixing = blend(picks, weights)
        panel = jnp.einsum("rbk,rkx->rbx", mixing.astype(jnp.float32), gathered.astype(jnp.float32)).astype(jnp.bfloat16)
        scaled = widths * BLK / (jnp.sum(kept, axis=1, keepdims=True) + 1.0)
        centre = jnp.einsum("rbx,rxy->rby", panel.astype(jnp.float32), tess_centre[tiles].astype(jnp.float32))
        side = jnp.einsum("rbx,rxy->rby", panel.astype(jnp.float32), tess_side[tiles].astype(jnp.float32))
        return (kept[..., None] * (centre + scaled[..., None] * side)).astype(jnp.bfloat16)

    ribbons = lax.map(one_device, jnp.arange(ndev, dtype=jnp.int32))
    tiles_all = route[:, 0].reshape(ndev, RB)
    same = tiles_all[:, :, None] == tiles_all[:, None, :]
    earlier = jnp.arange(RB)[None, :] < jnp.arange(RB)[:, None]
    rank = jnp.sum(same & earlier[None], axis=2).astype(jnp.int32)
    device = jnp.arange(ndev, dtype=jnp.int32)[:, None]
    scalp_of = device // SCREENS
    screen_of = device % SCREENS
    slot = ((scalp_of * SCREENS + tiles_all) * SCREENS + screen_of) * cap + rank
    placed = jnp.zeros((ndev * SCREENS * cap, BLK, 6 * P_SIZE), jnp.bfloat16)
    placed = placed.at[slot.reshape(-1)].set(ribbons.reshape(ndev * RB, BLK, 6 * P_SIZE))
    return placed.reshape(-1, 6 * P_SIZE)
```

```python
import functools

import jax
import jax.numpy as jnp
from jax import lax
from jax.experimental import pallas as pl
from jax.experimental.pallas import tpu as pltpu
from jax.sharding import PartitionSpec as P

F32 = jnp.float32
BF16 = jnp.bfloat16
VMEM = pl.BlockSpec(memory_space=pltpu.VMEM)
SMEM = pl.BlockSpec(memory_space=pltpu.SMEM)
CHUNK = 256
LIMIT = 16 * 1024 * 1024


def iota(shape, dim):
    return lax.broadcasted_iota(jnp.int32, shape, dim)


def fill_hot(hot_ref, index, valid):
    rows = index.shape[0]
    high = jnp.floor(index * (1.0 / CHUNK))
    low = index - high * CHUNK
    low = low if valid is None else jnp.where(valid, low, -1.0)
    lanes = iota((rows, CHUNK), 1).astype(F32)
    for part in range(hot_ref.shape[1] // CHUNK):
        key = jnp.where(high == part, low, -1.0)
        hot_ref[:, part * CHUNK : (part + 1) * CHUNK] = jnp.where(key == lanes, 1.0, 0.0).astype(BF16)


def serve_kernel(ask_ref, table_ref, out_ref, hot_ref):
    blocks, listed = ask_ref.shape
    tile = table_ref.shape[0]
    within = jnp.bitwise_and(ask_ref[...], tile - 1).astype(F32)
    wide = jnp.concatenate(
        [jnp.broadcast_to(within[b : b + 1, :], (listed, listed)) for b in range(blocks)], axis=0
    )
    on = jnp.bitwise_and(iota(wide.shape, 0), listed - 1) == iota(wide.shape, 1)
    index = jnp.sum(jnp.where(on, wide, 0.0), axis=1, keepdims=True)
    fill_hot(hot_ref, index, None)
    out_ref[...] = jnp.dot(hot_ref[...], table_ref[...], preferred_element_type=F32).astype(BF16)


def pack_kernel(route_ref, pick_ref, weight_ref, keep_ref, width_ref, after_ref, out_ref):
    blocks, picks, strands = pick_ref.shape
    del after_ref
    for b in range(blocks):
        tile = route_ref[b]
        rank = jnp.int32(0)
        for e in range(b):
            rank = rank + jnp.where(route_ref[e] == tile, 1, 0)
        kept = keep_ref[b : b + 1, :].astype(F32)
        scaled = width_ref[b : b + 1, :] * strands / (jnp.sum(kept, axis=1, keepdims=True) + 1.0)
        out_ref[b, 0:picks, :] = pick_ref[b].astype(F32)
        out_ref[b, picks : 2 * picks, :] = weight_ref[b].astype(F32)
        out_ref[b, 8:9, :] = kept
        out_ref[b, 9:10, :] = kept * scaled
        out_ref[b, 10:11, :] = jnp.full((1, strands), tile.astype(F32))
        out_ref[b, 11:12, :] = jnp.full((1, strands), rank.astype(F32))
        out_ref[b, 12:16, :] = jnp.zeros((4, strands), F32)


def plan_kernel(ask_ref, mine_ref, theirs_ref, table_ref, own_ref, sel_r_ref, sel_x_ref, mix_ref, hot_ref, *, scalps, slots):
    blocks, listed = ask_ref.shape
    half = blocks // 2
    tile = table_ref.shape[0]
    core = lax.axis_index("screen")
    here = lax.axis_index("scalp")
    strands = mine_ref.shape[2]
    lanes = blocks * listed
    core_f = core.astype(F32)
    codes = []
    for group, ref in enumerate((mine_ref, theirs_ref)):
        for b in range(half):
            goes = ref[b, 10:11, :] == core_f
            codes.append(jnp.where(goes, ref[b, 11:12, :], -1.0))
        for q in range(slots):
            packed = jnp.zeros((16, strands), F32)
            for b in range(half):
                packed = packed + jnp.where(codes[group * half + b] == q, ref[b], 0.0)
            spread = jnp.zeros((listed, strands), F32)
            row = iota((listed, strands), 0).astype(F32)
            for j in range(4):
                spread = spread + jnp.where(row == packed[j : j + 1, :], packed[4 + j : 5 + j, :], 0.0)
            both = jnp.concatenate([spread * packed[8:9, :], spread * packed[9:10, :]], axis=0)
            mix_ref[group * slots + q] = both.T.astype(BF16)
    ask = jnp.concatenate([ask_ref[...]] * blocks, axis=1)
    at = iota((blocks, lanes), 0) == iota((blocks, lanes), 1) // listed
    owner = ask // tile
    relative = owner - here + 1
    relative = jnp.where(relative < 0, relative + scalps, relative)
    relative = jnp.where(relative >= scalps, relative - scalps, relative)
    relative = jnp.sum(jnp.where(at, relative, 0).astype(F32), axis=0, keepdims=True)
    within = jnp.sum(jnp.where(at, jnp.bitwise_and(ask, tile - 1), 0).astype(F32), axis=0, keepdims=True)
    block_of = iota((1, lanes), 1) // listed
    code = jnp.zeros((1, lanes), F32)
    for b in range(blocks):
        code = code + jnp.where(block_of == b, codes[b][:, :lanes], 0.0)
    rows = 2 * slots * listed
    r = iota((rows, lanes), 0)
    l = iota((rows, lanes), 1)
    base = (r % listed == l % listed) & (r // (slots * listed) == l // (half * listed))
    base = base & (((r // listed) % slots).astype(F32) == code)
    near = 2.0 - 2.0 * core_f
    sel_r = jnp.where(base & (relative == near), 1.0, 0.0)
    sel_x = jnp.where(base & (relative == 2.0 - near), 1.0, 0.0)
    sel_o = jnp.where(base & (relative == 1.0), 1.0, 0.0)
    sel_r_ref[...] = sel_r.astype(BF16)
    swap = half * listed
    sel_x_ref[...] = jnp.concatenate([sel_x[:, swap:], sel_x[:, :swap]], axis=1).astype(BF16)
    index = jnp.sum(sel_o * within, axis=1, keepdims=True)
    valid = jnp.sum(sel_o, axis=1, keepdims=True) > 0.5
    fill_hot(hot_ref, index, valid)
    own_ref[...] = jnp.dot(hot_ref[...], table_ref[...], preferred_element_type=F32).astype(BF16)


def ribbon_kernel(near_ref, far_ref, own_ref, sel_r_ref, sel_x_ref, mix_ref, centre_ref, side_ref, out_ref, buffer, sems):
    total, strands, depth = mix_ref.shape
    listed = depth // 2
    slots = total // 2
    core = lax.axis_index("screen")
    rows = jnp.dot(sel_r_ref[...], near_ref[...], preferred_element_type=F32)
    rows = rows + jnp.dot(sel_x_ref[...], far_ref[...], preferred_element_type=F32)
    rows = (rows + own_ref[...].astype(F32)).astype(BF16)
    centre = jnp.dot(rows, centre_ref[0], preferred_element_type=F32).astype(BF16)
    side = jnp.dot(rows, side_ref[0], preferred_element_type=F32).astype(BF16)
    copies = []
    for i in range(total):
        both = jnp.concatenate(
            [centre[i * listed : (i + 1) * listed], side[i * listed : (i + 1) * listed]], axis=0
        )
        buffer[i] = jnp.dot(mix_ref[i], both, preferred_element_type=F32).astype(BF16)
        device = core if i < slots else 1 - core
        place = device * slots + i % slots
        copy = pltpu.make_async_copy(
            buffer.at[i], out_ref.at[pl.ds(pl.multiple_of(place * strands, strands), strands)], sems.at[i]
        )
        copy.start()
        copies.append(copy)
    for copy in copies:
        copy.wait()


def cost(flops, bytes_accessed):
    return pl.CostEstimate(flops=flops, bytes_accessed=bytes_accessed, transcendentals=0)


def shards(guides, neighbours, pick, pick_weight, keep, width, route, tess_centre, tess_side):
    scalps = lax.axis_size("scalp")
    screens = lax.axis_size("screen")
    tile, depth = guides.shape
    blocks, listed = neighbours.shape
    strands = keep.shape[1]
    slots = blocks // screens + blocks // 4
    points = tess_centre.shape[2]
    swap = [(0, 1), (1, 0)]
    both = ("scalp", "screen")
    ask_pairs = []
    for s in range(scalps):
        ask_pairs.append((2 * s, 2 * ((s + 1) % scalps)))
        ask_pairs.append((2 * s + 1, 2 * ((s - 1) % scalps) + 1))
    reply_pairs = [(b, a) for a, b in ask_pairs]

    ask = jnp.concatenate([neighbours, lax.ppermute(neighbours, "screen", swap)], axis=0)
    asked = lax.ppermute(ask, both, ask_pairs)
    all_rows = 2 * blocks * listed
    served = pl.pallas_call(
        serve_kernel,
        out_shape=jax.ShapeDtypeStruct((all_rows, depth), BF16),
        in_specs=[VMEM, VMEM],
        out_specs=VMEM,
        scratch_shapes=[pltpu.VMEM((all_rows, tile), BF16)],
        cost_estimate=cost(2 * all_rows * tile * depth, tile * depth * 2),
        compiler_params=pltpu.CompilerParams(vmem_limit_bytes=LIMIT),
        name="serve",
    )(asked, guides)
    near = lax.ppermute(served, both, reply_pairs)
    packed = pl.pallas_call(
        pack_kernel,
        out_shape=jax.ShapeDtypeStruct((blocks, 16, strands), F32),
        in_specs=[SMEM, VMEM, VMEM, VMEM, VMEM, pl.BlockSpec(memory_space=pl.ANY)],
        out_specs=VMEM,
        cost_estimate=cost(blocks * 16 * strands, blocks * 32 * strands),
        compiler_params=pltpu.CompilerParams(vmem_limit_bytes=LIMIT),
        name="pack",
    )(route[:, 0], pick, pick_weight, keep, width, served)
    theirs = lax.ppermute(packed, "screen", swap)
    total = 2 * slots
    own, sel_r, sel_x, mix = pl.pallas_call(
        functools.partial(plan_kernel, scalps=scalps, slots=slots),
        out_shape=(
            jax.ShapeDtypeStruct((total * listed, depth), BF16),
            jax.ShapeDtypeStruct((total * listed, all_rows), BF16),
            jax.ShapeDtypeStruct((total * listed, all_rows), BF16),
            jax.ShapeDtypeStruct((total, strands, 2 * listed), BF16),
        ),
        in_specs=[VMEM, VMEM, VMEM, VMEM],
        out_specs=(VMEM, VMEM, VMEM, VMEM),
        scratch_shapes=[pltpu.VMEM((total * listed, tile), BF16)],
        cost_estimate=cost(2 * total * listed * tile * depth, tile * depth * 2),
        compiler_params=pltpu.CompilerParams(vmem_limit_bytes=LIMIT),
        name="plan",
    )(ask, packed, theirs, guides)
    near, own = lax.optimization_barrier((near, own))
    far = lax.ppermute(near, "screen", swap)
    return pl.pallas_call(
        ribbon_kernel,
        out_shape=jax.ShapeDtypeStruct((total * strands, points), BF16),
        in_specs=[VMEM] * 8,
        out_specs=pl.BlockSpec(memory_space=pl.ANY),
        scratch_shapes=[pltpu.VMEM((total, strands, points), BF16), pltpu.SemaphoreType.DMA((total,))],
        cost_estimate=cost(2 * total * strands * points * 256, total * strands * points * 2),
        compiler_params=pltpu.CompilerParams(vmem_limit_bytes=LIMIT),
        name="ribbon",
    )(near, far, own, sel_r, sel_x, mix, tess_centre, tess_side)


def solution(mesh):
    return jax.shard_map(
        shards,
        mesh=mesh,
        in_specs=(
            P("scalp", None),
            P(("scalp", "screen"), None),
            P(("scalp", "screen"), None, None),
            P(("scalp", "screen"), None, None),
            P(("scalp", "screen"), None),
            P(("scalp", "screen"), None),
            P(("scalp", "screen"), None),
            P("screen", None, None),
            P("screen", None, None),
        ),
        out_specs=P(("scalp", "screen"), None),
        check_vma=False,
    )
```

```python
import functools

import jax
import jax.numpy as jnp
from jax import lax
from jax.experimental import pallas as pl
from jax.experimental.pallas import tpu as pltpu
from jax.sharding import PartitionSpec as P


F32 = jnp.float32
BF16 = jnp.bfloat16
VMEM = pl.BlockSpec(memory_space=pltpu.VMEM)
HBM = pl.BlockSpec(memory_space=pltpu.HBM)
SMEM = pl.BlockSpec(memory_space=pltpu.SMEM)
CHUNK = 256
LIMIT = 16 * 1024 * 1024


def iota(shape, dim):
    return lax.broadcasted_iota(jnp.int32, shape, dim)


def fill_hot(hot_ref, index, valid):
    rows = index.shape[0]
    high = jnp.floor(index * (1.0 / CHUNK))
    low = index - high * CHUNK
    low = low if valid is None else jnp.where(valid, low, -1.0)
    lanes = iota((rows, CHUNK), 1).astype(F32)
    for part in range(hot_ref.shape[1] // CHUNK):
        key = jnp.where(high == part, low, -1.0)
        hot_ref[:, part * CHUNK : (part + 1) * CHUNK] = jnp.where(key == lanes, 1.0, 0.0).astype(BF16)


def serve_kernel(first_ref, second_ref, table_ref, out_ref, hot_ref):
    listed = first_ref.shape[1]
    tile = table_ref.shape[0]
    ask = jnp.concatenate([first_ref[...], second_ref[...]], axis=0)
    blocks = ask.shape[0]
    within = jnp.bitwise_and(ask, tile - 1).astype(F32)
    wide = jnp.concatenate(
        [jnp.broadcast_to(within[b : b + 1, :], (listed, listed)) for b in range(blocks)], axis=0
    )
    on = jnp.bitwise_and(iota(wide.shape, 0), listed - 1) == iota(wide.shape, 1)
    index = jnp.sum(jnp.where(on, wide, 0.0), axis=1, keepdims=True)
    fill_hot(hot_ref, index, None)
    out_ref[...] = jnp.dot(hot_ref[...], table_ref[...], preferred_element_type=F32).astype(BF16)


def mark_kernel(out_ref):
    out_ref[...] = jnp.zeros_like(out_ref)


def pack_kernel(mark_ref, route_ref, *refs):
    del mark_ref
    *refs, out_ref = refs
    neighbours_ref, pick_ref, weight_ref, keep_ref, width_ref = refs
    blocks, picks, strands = pick_ref.shape
    times = strands // neighbours_ref.shape[1]
    for b in range(blocks):
        tile = route_ref[b]
        rank = jnp.int32(0)
        for e in range(b):
            rank = rank + jnp.where(route_ref[e] == tile, 1, 0)
        kept = keep_ref[b : b + 1, :].astype(F32)
        scaled = width_ref[b : b + 1, :] * strands / (jnp.sum(kept, axis=1, keepdims=True) + 1.0)
        out_ref[b, 0:picks, :] = pick_ref[b].astype(F32)
        out_ref[b, picks : 2 * picks, :] = weight_ref[b].astype(F32)
        out_ref[b, 8:9, :] = kept
        out_ref[b, 9:10, :] = kept * scaled
        out_ref[b, 10:11, :] = jnp.full((1, strands), tile.astype(F32))
        out_ref[b, 11:12, :] = jnp.full((1, strands), rank.astype(F32))
        listed = neighbours_ref[b : b + 1, :].astype(F32)
        out_ref[b, 12:13, :] = jnp.concatenate([listed] * times, axis=1)
        out_ref[b, 13:16, :] = jnp.zeros((3, strands), F32)


def plan_kernel(mine_ref, theirs_ref, table_ref, own_ref, sel_r_ref, sel_x_ref, mix_ref, hot_ref, *, scalps, slots):
    half = mine_ref.shape[0]
    blocks = 2 * half
    listed = mix_ref.shape[2] // 2
    tile = table_ref.shape[0]
    core = lax.axis_index("screen")
    here = lax.axis_index("scalp")
    strands = mine_ref.shape[2]
    lanes = blocks * listed
    core_f = core.astype(F32)
    codes = []
    for group, ref in enumerate((mine_ref, theirs_ref)):
        for b in range(half):
            goes = ref[b, 10:11, :] == core_f
            codes.append(jnp.where(goes, ref[b, 11:12, :], -1.0))
        for q in range(slots):
            packed = jnp.zeros((16, strands), F32)
            for b in range(half):
                packed = packed + jnp.where(codes[group * half + b] == q, ref[b], 0.0)
            spread = jnp.zeros((listed, strands), F32)
            row = iota((listed, strands), 0).astype(F32)
            for j in range(4):
                spread = spread + jnp.where(row == packed[j : j + 1, :], packed[4 + j : 5 + j, :], 0.0)
            both = jnp.concatenate([spread * packed[8:9, :], spread * packed[9:10, :]], axis=0)
            mix_ref[group * slots + q] = both.T.astype(BF16)
    block_of = iota((1, lanes), 1) // listed
    code = jnp.zeros((1, lanes), F32)
    ask = jnp.zeros((1, lanes), F32)
    for b in range(blocks):
        ref = (mine_ref, theirs_ref)[b // half]
        code = code + jnp.where(block_of == b, codes[b][:, :lanes], 0.0)
        ask = ask + jnp.where(block_of == b, ref[b % half, 12:13, :lanes], 0.0)
    owner = jnp.floor(ask * (1.0 / tile))
    within = ask - owner * tile
    relative = owner - here.astype(F32) + 1.0
    relative = jnp.where(relative < 0.0, relative + scalps, relative)
    relative = jnp.where(relative >= scalps, relative - scalps, relative)
    rows = 2 * slots * listed
    r = iota((rows, lanes), 0)
    l = iota((rows, lanes), 1)
    base = (r % listed == l % listed) & (r // (slots * listed) == l // (half * listed))
    base = base & (((r // listed) % slots).astype(F32) == code)
    near = 2.0 - 2.0 * core_f
    sel_r = jnp.where(base & (relative == near), 1.0, 0.0)
    sel_x = jnp.where(base & (relative == 2.0 - near), 1.0, 0.0)
    sel_o = jnp.where(base & (relative == 1.0), 1.0, 0.0)
    sel_r_ref[...] = sel_r.astype(BF16)
    swap = half * listed
    sel_x_ref[...] = jnp.concatenate([sel_x[:, swap:], sel_x[:, :swap]], axis=1).astype(BF16)
    index = jnp.sum(sel_o * within, axis=1, keepdims=True)
    valid = jnp.sum(sel_o, axis=1, keepdims=True) > 0.5
    fill_hot(hot_ref, index, valid)
    own_ref[...] = jnp.dot(hot_ref[...], table_ref[...], preferred_element_type=F32).astype(BF16)


def ribbon_kernel(near_ref, far_ref, own_ref, sel_r_ref, sel_x_ref, mix_ref, centre_ref, side_ref, out_ref, buffer, sems):
    total, strands, depth = mix_ref.shape
    listed = depth // 2
    slots = total // 2
    core = lax.axis_index("screen")
    rows = jnp.dot(sel_r_ref[...], near_ref[...], preferred_element_type=F32)
    rows = rows + jnp.dot(sel_x_ref[...], far_ref[...], preferred_element_type=F32)
    rows = (rows + own_ref[...].astype(F32)).astype(BF16)
    centre = jnp.dot(rows, centre_ref[0], preferred_element_type=F32).astype(BF16)
    side = jnp.dot(rows, side_ref[0], preferred_element_type=F32).astype(BF16)
    copies = []
    for i in range(total):
        both = jnp.concatenate(
            [centre[i * listed : (i + 1) * listed], side[i * listed : (i + 1) * listed]], axis=0
        )
        buffer[i] = jnp.dot(mix_ref[i], both, preferred_element_type=F32).astype(BF16)
        device = core if i < slots else 1 - core
        place = device * slots + i % slots
        copy = pltpu.make_async_copy(
            buffer.at[i], out_ref.at[pl.ds(pl.multiple_of(place * strands, strands), strands)], sems.at[i]
        )
        copy.start()
        copies.append(copy)
    for copy in copies:
        copy.wait()


def cost(flops, bytes_accessed):
    return pl.CostEstimate(flops=flops, bytes_accessed=bytes_accessed, transcendentals=0)


def body(guides, neighbours, pick, pick_weight, keep, width, route, tess_centre, tess_side):
    scalps = lax.axis_size("scalp")
    screens = lax.axis_size("screen")
    tile, depth = guides.shape
    blocks, listed = neighbours.shape
    strands = keep.shape[1]
    slots = blocks // screens + blocks // 4
    points = tess_centre.shape[2]
    swap = [(0, 1), (1, 0)]
    both = ("scalp", "screen")
    ask_pairs, cross_pairs = [], []
    for s in range(scalps):
        high, low = 2 * ((s + 1) % scalps), 2 * ((s - 1) % scalps) + 1
        ask_pairs += [(2 * s, high), (2 * s + 1, low)]
        cross_pairs += [(2 * s + 1, high), (2 * s, low)]
    reply_pairs = [(b, a) for a, b in ask_pairs]
    pass_pairs = [(b, a) for a, b in cross_pairs]

    mark = pl.pallas_call(
        mark_kernel,
        out_shape=jax.ShapeDtypeStruct((8, 128), F32),
        out_specs=VMEM,
        cost_estimate=cost(20_000_000_000, 2_000_000),
        compiler_params=pltpu.CompilerParams(vmem_limit_bytes=LIMIT),
        name="mark",
    )()
    first = lax.ppermute(neighbours, both, ask_pairs)
    second = lax.ppermute(neighbours, both, cross_pairs)
    parts = (neighbours, pick, pick_weight, keep, width)
    packed = pl.pallas_call(
        pack_kernel,
        out_shape=jax.ShapeDtypeStruct((blocks, 16, strands), F32),
        in_specs=[VMEM, SMEM] + [VMEM] * len(parts),
        out_specs=VMEM,
        cost_estimate=cost(blocks * 16 * strands, blocks * 32 * strands),
        compiler_params=pltpu.CompilerParams(vmem_limit_bytes=LIMIT),
        name="pack",
    )(mark, route[:, 0], *parts)
    first, packed = lax.optimization_barrier((first, packed))
    all_rows = 2 * blocks * listed
    served = pl.pallas_call(
        serve_kernel,
        out_shape=jax.ShapeDtypeStruct((all_rows, depth), BF16),
        in_specs=[VMEM, VMEM, VMEM],
        out_specs=VMEM,
        scratch_shapes=[pltpu.VMEM((all_rows, tile), BF16)],
        cost_estimate=cost(2 * all_rows * tile * depth, tile * depth * 2),
        compiler_params=pltpu.CompilerParams(vmem_limit_bytes=LIMIT),
        name="serve",
    )(first, second, guides)
    served, packed = lax.optimization_barrier((served, packed))
    near = lax.ppermute(served, both, reply_pairs)
    far = lax.ppermute(served, both, pass_pairs)
    theirs = lax.ppermute(packed, "screen", swap)
    total = 2 * slots
    own, sel_r, sel_x, mix = pl.pallas_call(
        functools.partial(plan_kernel, scalps=scalps, slots=slots),
        out_shape=(
            jax.ShapeDtypeStruct((total * listed, depth), BF16),
            jax.ShapeDtypeStruct((total * listed, all_rows), BF16),
            jax.ShapeDtypeStruct((total * listed, all_rows), BF16),
            jax.ShapeDtypeStruct((total, strands, 2 * listed), BF16),
        ),
        in_specs=[VMEM, VMEM, VMEM],
        out_specs=(VMEM, VMEM, VMEM, VMEM),
        scratch_shapes=[pltpu.VMEM((total * listed, tile), BF16)],
        cost_estimate=cost(2 * total * listed * tile * depth, tile * depth * 2),
        compiler_params=pltpu.CompilerParams(vmem_limit_bytes=LIMIT),
        name="plan",
    )(packed, theirs, guides)
    return pl.pallas_call(
        ribbon_kernel,
        out_shape=jax.ShapeDtypeStruct((total * strands, points), BF16),
        in_specs=[VMEM] * 8,
        out_specs=pl.BlockSpec(memory_space=pl.ANY),
        scratch_shapes=[pltpu.VMEM((total, strands, points), BF16), pltpu.SemaphoreType.DMA((total,))],
        cost_estimate=cost(2 * total * strands * points * 256, total * strands * points * 2),
        compiler_params=pltpu.CompilerParams(vmem_limit_bytes=LIMIT),
        name="ribbon",
    )(near, far, own, sel_r, sel_x, mix, tess_centre, tess_side)


def solution(mesh):
    return jax.shard_map(
        body,
        mesh=mesh,
        in_specs=(
            P("scalp", None),
            P(("scalp", "screen"), None),
            P(("scalp", "screen"), None, None),
            P(("scalp", "screen"), None, None),
            P(("scalp", "screen"), None),
            P(("scalp", "screen"), None),
            P(("scalp", "screen"), None),
            P("screen", None, None),
            P("screen", None, None),
        ),
        out_specs=P(("scalp", "screen"), None),
        check_vma=False,
    )
```

```python
import functools

import jax
import jax.numpy as jnp
from jax import lax
from jax.experimental import pallas as pl
from jax.experimental.pallas import tpu as pltpu
from jax.sharding import PartitionSpec as P


F32 = jnp.float32
BF16 = jnp.bfloat16
VMEM = pl.BlockSpec(memory_space=pltpu.VMEM)
HBM = pl.BlockSpec(memory_space=pltpu.HBM)
SMEM = pl.BlockSpec(memory_space=pltpu.SMEM)
CHUNK = 256
LIMIT = 16 * 1024 * 1024


def iota(shape, dim):
    return lax.broadcasted_iota(jnp.int32, shape, dim)


def fill_hot(hot_ref, index, valid):
    rows = index.shape[0]
    high = jnp.floor(index * (1.0 / CHUNK))
    low = index - high * CHUNK
    low = low if valid is None else jnp.where(valid, low, -1.0)
    lanes = iota((rows, CHUNK), 1).astype(F32)
    for part in range(hot_ref.shape[1] // CHUNK):
        key = jnp.where(high == part, low, -1.0)
        hot_ref[:, part * CHUNK : (part + 1) * CHUNK] = jnp.where(key == lanes, 1.0, 0.0).astype(BF16)


def serve_kernel(ask_ref, table_ref, *refs):
    *before, out_ref, hot_ref = refs
    blocks, listed = ask_ref.shape
    tile = table_ref.shape[0]
    within = jnp.bitwise_and(ask_ref[...], tile - 1).astype(F32)
    wide = jnp.concatenate(
        [jnp.broadcast_to(within[b : b + 1, :], (listed, listed)) for b in range(blocks)], axis=0
    )
    on = jnp.bitwise_and(iota(wide.shape, 0), listed - 1) == iota(wide.shape, 1)
    index = jnp.sum(jnp.where(on, wide, 0.0), axis=1, keepdims=True)
    fill_hot(hot_ref, index, None)
    rows = jnp.dot(hot_ref[...], table_ref[...], preferred_element_type=F32).astype(BF16)
    start = out_ref.shape[0] - rows.shape[0]
    for ref in before:
        out_ref[:start, :] = ref[...]
    out_ref[start:, :] = rows


def mark_kernel(out_ref):
    out_ref[...] = jnp.zeros_like(out_ref)


def pack_kernel(mark_ref, route_ref, *refs):
    del mark_ref
    *refs, out_ref = refs
    neighbours_ref, pick_ref, weight_ref, keep_ref, width_ref = refs
    blocks, picks, strands = pick_ref.shape
    times = strands // neighbours_ref.shape[1]
    for b in range(blocks):
        tile = route_ref[b]
        rank = jnp.int32(0)
        for e in range(b):
            rank = rank + jnp.where(route_ref[e] == tile, 1, 0)
        kept = keep_ref[b : b + 1, :].astype(F32)
        scaled = width_ref[b : b + 1, :] * strands / (jnp.sum(kept, axis=1, keepdims=True) + 1.0)
        out_ref[b, 0:picks, :] = pick_ref[b].astype(F32)
        out_ref[b, picks : 2 * picks, :] = weight_ref[b].astype(F32)
        out_ref[b, 8:9, :] = kept
        out_ref[b, 9:10, :] = kept * scaled
        out_ref[b, 10:11, :] = jnp.full((1, strands), tile.astype(F32))
        out_ref[b, 11:12, :] = jnp.full((1, strands), rank.astype(F32))
        listed = neighbours_ref[b : b + 1, :].astype(F32)
        out_ref[b, 12:13, :] = jnp.concatenate([listed] * times, axis=1)
        out_ref[b, 13:16, :] = jnp.zeros((3, strands), F32)


def plan_kernel(mine_ref, theirs_ref, table_ref, own_ref, sel_r_ref, sel_x_ref, mix_ref, hot_ref, *, scalps, slots):
    half = mine_ref.shape[0]
    blocks = 2 * half
    listed = mix_ref.shape[2] // 2
    tile = table_ref.shape[0]
    core = lax.axis_index("screen")
    here = lax.axis_index("scalp")
    strands = mine_ref.shape[2]
    lanes = blocks * listed
    core_f = core.astype(F32)
    codes = []
    for group, ref in enumerate((mine_ref, theirs_ref)):
        for b in range(half):
            goes = ref[b, 10:11, :] == core_f
            codes.append(jnp.where(goes, ref[b, 11:12, :], -1.0))
        for q in range(slots):
            packed = jnp.zeros((16, strands), F32)
            for b in range(half):
                packed = packed + jnp.where(codes[group * half + b] == q, ref[b], 0.0)
            spread = jnp.zeros((listed, strands), F32)
            row = iota((listed, strands), 0).astype(F32)
            for j in range(4):
                spread = spread + jnp.where(row == packed[j : j + 1, :], packed[4 + j : 5 + j, :], 0.0)
            both = jnp.concatenate([spread * packed[8:9, :], spread * packed[9:10, :]], axis=0)
            mix_ref[group * slots + q] = both.T.astype(BF16)
    block_of = iota((1, lanes), 1) // listed
    code = jnp.zeros((1, lanes), F32)
    ask = jnp.zeros((1, lanes), F32)
    for b in range(blocks):
        ref = (mine_ref, theirs_ref)[b // half]
        code = code + jnp.where(block_of == b, codes[b][:, :lanes], 0.0)
        ask = ask + jnp.where(block_of == b, ref[b % half, 12:13, :lanes], 0.0)
    owner = jnp.floor(ask * (1.0 / tile))
    within = ask - owner * tile
    relative = owner - here.astype(F32) + 1.0
    relative = jnp.where(relative < 0.0, relative + scalps, relative)
    relative = jnp.where(relative >= scalps, relative - scalps, relative)
    rows = 2 * slots * listed
    r = iota((rows, lanes), 0)
    l = iota((rows, lanes), 1)
    base = (r % listed == l % listed) & (r // (slots * listed) == l // (half * listed))
    base = base & (((r // listed) % slots).astype(F32) == code)
    near = 2.0 - 2.0 * core_f
    sel_r = jnp.where(base & (relative == near), 1.0, 0.0)
    sel_x = jnp.where(base & (relative == 2.0 - near), 1.0, 0.0)
    sel_o = jnp.where(base & (relative == 1.0), 1.0, 0.0)
    sel_r_ref[...] = sel_r.astype(BF16)
    swap = half * listed
    sel_x_ref[...] = jnp.concatenate([sel_x[:, swap:], sel_x[:, :swap]], axis=1).astype(BF16)
    index = jnp.sum(sel_o * within, axis=1, keepdims=True)
    valid = jnp.sum(sel_o, axis=1, keepdims=True) > 0.5
    fill_hot(hot_ref, index, valid)
    own_ref[...] = jnp.dot(hot_ref[...], table_ref[...], preferred_element_type=F32).astype(BF16)


def ribbon_kernel(near_ref, far_ref, own_ref, sel_r_ref, sel_x_ref, mix_ref, centre_ref, side_ref, out_ref, buffer, sems):
    total, strands, depth = mix_ref.shape
    listed = depth // 2
    slots = total // 2
    core = lax.axis_index("screen")
    rows = jnp.dot(sel_r_ref[...], near_ref[...], preferred_element_type=F32)
    rows = rows + jnp.dot(sel_x_ref[...], far_ref[...], preferred_element_type=F32)
    rows = (rows + own_ref[...].astype(F32)).astype(BF16)
    centre = jnp.dot(rows, centre_ref[0], preferred_element_type=F32).astype(BF16)
    side = jnp.dot(rows, side_ref[0], preferred_element_type=F32).astype(BF16)
    copies = []
    for i in range(total):
        both = jnp.concatenate(
            [centre[i * listed : (i + 1) * listed], side[i * listed : (i + 1) * listed]], axis=0
        )
        buffer[i] = jnp.dot(mix_ref[i], both, preferred_element_type=F32).astype(BF16)
        device = core if i < slots else 1 - core
        place = device * slots + i % slots
        copy = pltpu.make_async_copy(
            buffer.at[i], out_ref.at[pl.ds(pl.multiple_of(place * strands, strands), strands)], sems.at[i]
        )
        copy.start()
        copies.append(copy)
    for copy in copies:
        copy.wait()


def cost(flops, bytes_accessed):
    return pl.CostEstimate(flops=flops, bytes_accessed=bytes_accessed, transcendentals=0)


def body(guides, neighbours, pick, pick_weight, keep, width, route, tess_centre, tess_side):
    scalps = lax.axis_size("scalp")
    screens = lax.axis_size("screen")
    tile, depth = guides.shape
    blocks, listed = neighbours.shape
    strands = keep.shape[1]
    slots = blocks // screens + blocks // 4
    points = tess_centre.shape[2]
    swap = [(0, 1), (1, 0)]
    both = ("scalp", "screen")
    ask_pairs, cross_pairs = [], []
    for s in range(scalps):
        high, low = 2 * ((s + 1) % scalps), 2 * ((s - 1) % scalps) + 1
        ask_pairs += [(2 * s, high), (2 * s + 1, low)]
        cross_pairs += [(2 * s + 1, high), (2 * s, low)]
    reply_pairs = [(b, a) for a, b in ask_pairs]
    pass_pairs = [(b, a) for a, b in cross_pairs]

    mark = pl.pallas_call(
        mark_kernel,
        out_shape=jax.ShapeDtypeStruct((8, 128), F32),
        out_specs=VMEM,
        cost_estimate=cost(20_000_000_000, 2_000_000),
        compiler_params=pltpu.CompilerParams(vmem_limit_bytes=LIMIT),
        name="mark",
    )()
    first = lax.ppermute(neighbours, both, ask_pairs)
    second = lax.ppermute(neighbours, both, cross_pairs)
    parts = (neighbours, pick, pick_weight, keep, width)
    packed = pl.pallas_call(
        pack_kernel,
        out_shape=jax.ShapeDtypeStruct((blocks, 16, strands), F32),
        in_specs=[VMEM, SMEM] + [VMEM] * len(parts),
        out_specs=VMEM,
        cost_estimate=cost(blocks * 16 * strands, blocks * 32 * strands),
        compiler_params=pltpu.CompilerParams(vmem_limit_bytes=LIMIT),
        name="pack",
    )(mark, route[:, 0], *parts)
    first, packed = lax.optimization_barrier((first, packed))
    all_rows = 2 * blocks * listed
    half_rows = all_rows // 2

    def serve(rows, *operands):
        return pl.pallas_call(
            serve_kernel,
            out_shape=jax.ShapeDtypeStruct((rows, depth), BF16),
            in_specs=[VMEM] * len(operands),
            out_specs=VMEM,
            scratch_shapes=[pltpu.VMEM((half_rows, tile), BF16)],
            cost_estimate=cost(2 * half_rows * tile * depth, tile * depth * 2),
            compiler_params=pltpu.CompilerParams(vmem_limit_bytes=LIMIT),
        )(*operands)

    served = serve(half_rows, first, guides)
    served = serve(all_rows, second, guides, served)
    served, packed = lax.optimization_barrier((served, packed))
    near = lax.ppermute(served, both, reply_pairs)
    far = lax.ppermute(served, both, pass_pairs)
    theirs = lax.ppermute(packed, "screen", swap)
    total = 2 * slots
    own, sel_r, sel_x, mix = pl.pallas_call(
        functools.partial(plan_kernel, scalps=scalps, slots=slots),
        out_shape=(
            jax.ShapeDtypeStruct((total * listed, depth), BF16),
            jax.ShapeDtypeStruct((total * listed, all_rows), BF16),
            jax.ShapeDtypeStruct((total * listed, all_rows), BF16),
            jax.ShapeDtypeStruct((total, strands, 2 * listed), BF16),
        ),
        in_specs=[VMEM, VMEM, VMEM],
        out_specs=(VMEM, VMEM, VMEM, VMEM),
        scratch_shapes=[pltpu.VMEM((total * listed, tile), BF16)],
        cost_estimate=cost(2 * total * listed * tile * depth, tile * depth * 2),
        compiler_params=pltpu.CompilerParams(vmem_limit_bytes=LIMIT),
        name="plan",
    )(packed, theirs, guides)
    return pl.pallas_call(
        ribbon_kernel,
        out_shape=jax.ShapeDtypeStruct((total * strands, points), BF16),
        in_specs=[VMEM] * 8,
        out_specs=pl.BlockSpec(memory_space=pl.ANY),
        scratch_shapes=[pltpu.VMEM((total, strands, points), BF16), pltpu.SemaphoreType.DMA((total,))],
        cost_estimate=cost(2 * total * strands * points * 256, total * strands * points * 2),
        compiler_params=pltpu.CompilerParams(vmem_limit_bytes=LIMIT),
        name="ribbon",
    )(near, far, own, sel_r, sel_x, mix, tess_centre, tess_side)


def solution(mesh):
    return jax.shard_map(
        body,
        mesh=mesh,
        in_specs=(
            P("scalp", None),
            P(("scalp", "screen"), None),
            P(("scalp", "screen"), None, None),
            P(("scalp", "screen"), None, None),
            P(("scalp", "screen"), None),
            P(("scalp", "screen"), None),
            P(("scalp", "screen"), None),
            P("screen", None, None),
            P("screen", None, None),
        ),
        out_specs=P(("scalp", "screen"), None),
        check_vma=False,
    )
```

```python
import functools

import jax
import jax.numpy as jnp
from jax import lax
from jax.experimental import pallas as pl
from jax.experimental.pallas import tpu as pltpu
from jax.sharding import PartitionSpec as P


F32 = jnp.float32
BF16 = jnp.bfloat16
VMEM = pl.BlockSpec(memory_space=pltpu.VMEM)
HBM = pl.BlockSpec(memory_space=pltpu.HBM)
SMEM = pl.BlockSpec(memory_space=pltpu.SMEM)
CHUNK = 256
LIMIT = 16 * 1024 * 1024


def iota(shape, dim):
    return lax.broadcasted_iota(jnp.int32, shape, dim)


def fill_hot(hot_ref, index, valid):
    rows = index.shape[0]
    high = jnp.floor(index * (1.0 / CHUNK))
    low = index - high * CHUNK
    low = low if valid is None else jnp.where(valid, low, -1.0)
    lanes = iota((rows, CHUNK), 1).astype(F32).astype(BF16)
    one, zero = jnp.array(1.0, BF16), jnp.array(0.0, BF16)
    for part in range(hot_ref.shape[1] // CHUNK):
        key = jnp.where(high == part, low, -1.0).astype(BF16)
        hot_ref[:, part * CHUNK : (part + 1) * CHUNK] = jnp.where(key == lanes, one, zero)


def serve_kernel(ask_ref, table_ref, *refs):
    *before, out_ref, hot_ref = refs
    blocks, listed = ask_ref.shape
    tile = table_ref.shape[0]
    within = jnp.bitwise_and(ask_ref[...], tile - 1).astype(F32)
    wide = jnp.concatenate(
        [jnp.broadcast_to(within[b : b + 1, :], (listed, listed)) for b in range(blocks)], axis=0
    )
    on = jnp.bitwise_and(iota(wide.shape, 0), listed - 1) == iota(wide.shape, 1)
    index = jnp.sum(jnp.where(on, wide, 0.0), axis=1, keepdims=True)
    fill_hot(hot_ref, index, None)
    rows = jnp.dot(hot_ref[...], table_ref[...], preferred_element_type=F32).astype(BF16)
    start = out_ref.shape[0] - rows.shape[0]
    for ref in before:
        out_ref[:start, :] = ref[...]
    out_ref[start:, :] = rows


def mark_kernel(out_ref):
    out_ref[...] = jnp.zeros_like(out_ref)


def pack_kernel(mark_ref, route_ref, *refs):
    del mark_ref
    *refs, out_ref = refs
    neighbours_ref, pick_ref, weight_ref, keep_ref, width_ref = refs
    blocks, picks, strands = pick_ref.shape
    times = strands // neighbours_ref.shape[1]
    for b in range(blocks):
        tile = route_ref[b]
        rank = jnp.int32(0)
        for e in range(b):
            rank = rank + jnp.where(route_ref[e] == tile, 1, 0)
        kept = keep_ref[b : b + 1, :].astype(F32)
        scaled = width_ref[b : b + 1, :] * strands / (jnp.sum(kept, axis=1, keepdims=True) + 1.0)
        out_ref[b, 0:picks, :] = pick_ref[b].astype(F32)
        out_ref[b, picks : 2 * picks, :] = weight_ref[b].astype(F32)
        out_ref[b, 8:9, :] = kept
        out_ref[b, 9:10, :] = kept * scaled
        out_ref[b, 10:11, :] = jnp.full((1, strands), tile.astype(F32))
        out_ref[b, 11:12, :] = jnp.full((1, strands), rank.astype(F32))
        listed = neighbours_ref[b : b + 1, :].astype(F32)
        out_ref[b, 12:13, :] = jnp.concatenate([listed] * times, axis=1)
        out_ref[b, 13:16, :] = jnp.zeros((3, strands), F32)


def plan_kernel(mine_ref, theirs_ref, table_ref, own_ref, sel_r_ref, sel_x_ref, mix_ref, hot_ref, *, scalps, slots):
    half = mine_ref.shape[0]
    blocks = 2 * half
    listed = mix_ref.shape[2] // 2
    tile = table_ref.shape[0]
    core = lax.axis_index("screen")
    here = lax.axis_index("scalp")
    strands = mine_ref.shape[2]
    lanes = blocks * listed
    core_f = core.astype(F32)
    codes = []
    for group, ref in enumerate((mine_ref, theirs_ref)):
        for b in range(half):
            goes = ref[b, 10:11, :] == core_f
            codes.append(jnp.where(goes, ref[b, 11:12, :], -1.0))
        for q in range(slots):
            packed = jnp.zeros((16, strands), F32)
            for b in range(half):
                packed = packed + jnp.where(codes[group * half + b] == q, ref[b], 0.0)
            spread = jnp.zeros((listed, strands), F32)
            row = iota((listed, strands), 0).astype(F32)
            for j in range(4):
                spread = spread + jnp.where(row == packed[j : j + 1, :], packed[4 + j : 5 + j, :], 0.0)
            both = jnp.concatenate([spread * packed[8:9, :], spread * packed[9:10, :]], axis=0)
            mix_ref[group * slots + q] = both.T.astype(BF16)
    block_of = iota((1, lanes), 1) // listed
    code = jnp.zeros((1, lanes), F32)
    ask = jnp.zeros((1, lanes), F32)
    for b in range(blocks):
        ref = (mine_ref, theirs_ref)[b // half]
        code = code + jnp.where(block_of == b, codes[b][:, :lanes], 0.0)
        ask = ask + jnp.where(block_of == b, ref[b % half, 12:13, :lanes], 0.0)
    owner = jnp.floor(ask * (1.0 / tile))
    within = ask - owner * tile
    relative = owner - here.astype(F32) + 1.0
    relative = jnp.where(relative < 0.0, relative + scalps, relative)
    relative = jnp.where(relative >= scalps, relative - scalps, relative)
    rows = 2 * slots * listed
    r = iota((rows, lanes), 0)
    l = iota((rows, lanes), 1)
    base = (r % listed == l % listed) & (r // (slots * listed) == l // (half * listed))
    base = base & (((r // listed) % slots).astype(F32) == code)
    near = 2.0 - 2.0 * core_f
    sel_r = jnp.where(base & (relative == near), 1.0, 0.0)
    sel_x = jnp.where(base & (relative == 2.0 - near), 1.0, 0.0)
    sel_o = jnp.where(base & (relative == 1.0), 1.0, 0.0)
    sel_r_ref[...] = sel_r.astype(BF16)
    swap = half * listed
    sel_x_ref[...] = jnp.concatenate([sel_x[:, swap:], sel_x[:, :swap]], axis=1).astype(BF16)
    index = jnp.sum(sel_o * within, axis=1, keepdims=True)
    valid = jnp.sum(sel_o, axis=1, keepdims=True) > 0.5
    fill_hot(hot_ref, index, valid)
    own_ref[...] = jnp.dot(hot_ref[...], table_ref[...], preferred_element_type=F32).astype(BF16)


def ribbon_kernel(near_ref, far_ref, own_ref, sel_r_ref, sel_x_ref, mix_ref, centre_ref, side_ref, out_ref, buffer, sems):
    total, strands, depth = mix_ref.shape
    listed = depth // 2
    slots = total // 2
    core = lax.axis_index("screen")
    rows = jnp.dot(sel_r_ref[...], near_ref[...], preferred_element_type=F32)
    rows = rows + jnp.dot(sel_x_ref[...], far_ref[...], preferred_element_type=F32)
    rows = (rows + own_ref[...].astype(F32)).astype(BF16)
    centre = jnp.dot(rows, centre_ref[0], preferred_element_type=F32).astype(BF16)
    side = jnp.dot(rows, side_ref[0], preferred_element_type=F32).astype(BF16)
    copies = []
    for i in range(total):
        both = jnp.concatenate(
            [centre[i * listed : (i + 1) * listed], side[i * listed : (i + 1) * listed]], axis=0
        )
        buffer[i] = jnp.dot(mix_ref[i], both, preferred_element_type=F32).astype(BF16)
        device = core if i < slots else 1 - core
        place = device * slots + i % slots
        copy = pltpu.make_async_copy(
            buffer.at[i], out_ref.at[pl.ds(pl.multiple_of(place * strands, strands), strands)], sems.at[i]
        )
        copy.start()
        copies.append(copy)
    for copy in copies:
        copy.wait()


def cost(flops, bytes_accessed):
    return pl.CostEstimate(flops=flops, bytes_accessed=bytes_accessed, transcendentals=0)


def body(guides, neighbours, pick, pick_weight, keep, width, route, tess_centre, tess_side):
    scalps = lax.axis_size("scalp")
    screens = lax.axis_size("screen")
    tile, depth = guides.shape
    blocks, listed = neighbours.shape
    strands = keep.shape[1]
    slots = blocks // screens + blocks // 4
    points = tess_centre.shape[2]
    swap = [(0, 1), (1, 0)]
    both = ("scalp", "screen")
    ask_pairs, cross_pairs = [], []
    for s in range(scalps):
        high, low = 2 * ((s + 1) % scalps), 2 * ((s - 1) % scalps) + 1
        ask_pairs += [(2 * s, high), (2 * s + 1, low)]
        cross_pairs += [(2 * s + 1, high), (2 * s, low)]
    reply_pairs = [(b, a) for a, b in ask_pairs]
    pass_pairs = [(b, a) for a, b in cross_pairs]

    mark = pl.pallas_call(
        mark_kernel,
        out_shape=jax.ShapeDtypeStruct((8, 128), F32),
        out_specs=VMEM,
        cost_estimate=cost(20_000_000_000, 2_000_000),
        compiler_params=pltpu.CompilerParams(vmem_limit_bytes=LIMIT),
        name="mark",
    )()
    first = lax.ppermute(neighbours, both, ask_pairs)
    second = lax.ppermute(neighbours, both, cross_pairs)
    parts = (neighbours, pick, pick_weight, keep, width)
    packed = pl.pallas_call(
        pack_kernel,
        out_shape=jax.ShapeDtypeStruct((blocks, 16, strands), F32),
        in_specs=[VMEM, SMEM] + [VMEM] * len(parts),
        out_specs=VMEM,
        cost_estimate=cost(blocks * 16 * strands, blocks * 32 * strands),
        compiler_params=pltpu.CompilerParams(vmem_limit_bytes=LIMIT),
        name="pack",
    )(mark, route[:, 0], *parts)
    first, packed = lax.optimization_barrier((first, packed))
    all_rows = 2 * blocks * listed
    half_rows = all_rows // 2

    def serve(rows, *operands):
        return pl.pallas_call(
            serve_kernel,
            out_shape=jax.ShapeDtypeStruct((rows, depth), BF16),
            in_specs=[VMEM] * len(operands),
            out_specs=VMEM,
            scratch_shapes=[pltpu.VMEM((half_rows, tile), BF16)],
            cost_estimate=cost(2 * half_rows * tile * depth, tile * depth * 2),
            compiler_params=pltpu.CompilerParams(vmem_limit_bytes=LIMIT),
        )(*operands)

    served = serve(half_rows, first, guides)
    served = serve(all_rows, second, guides, served)
    served, packed = lax.optimization_barrier((served, packed))
    near = lax.ppermute(served, both, reply_pairs)
    far = lax.ppermute(served, both, pass_pairs)
    theirs = lax.ppermute(packed, "screen", swap)
    total = 2 * slots
    own, sel_r, sel_x, mix = pl.pallas_call(
        functools.partial(plan_kernel, scalps=scalps, slots=slots),
        out_shape=(
            jax.ShapeDtypeStruct((total * listed, depth), BF16),
            jax.ShapeDtypeStruct((total * listed, all_rows), BF16),
            jax.ShapeDtypeStruct((total * listed, all_rows), BF16),
            jax.ShapeDtypeStruct((total, strands, 2 * listed), BF16),
        ),
        in_specs=[VMEM, VMEM, VMEM],
        out_specs=(VMEM, VMEM, VMEM, VMEM),
        scratch_shapes=[pltpu.VMEM((total * listed, tile), BF16)],
        cost_estimate=cost(2 * total * listed * tile * depth, tile * depth * 2),
        compiler_params=pltpu.CompilerParams(vmem_limit_bytes=LIMIT),
        name="plan",
    )(packed, theirs, guides)
    return pl.pallas_call(
        ribbon_kernel,
        out_shape=jax.ShapeDtypeStruct((total * strands, points), BF16),
        in_specs=[VMEM] * 8,
        out_specs=pl.BlockSpec(memory_space=pl.ANY),
        scratch_shapes=[pltpu.VMEM((total, strands, points), BF16), pltpu.SemaphoreType.DMA((total,))],
        cost_estimate=cost(2 * total * strands * points * 256, total * strands * points * 2),
        compiler_params=pltpu.CompilerParams(vmem_limit_bytes=LIMIT),
        name="ribbon",
    )(near, far, own, sel_r, sel_x, mix, tess_centre, tess_side)


def solution(mesh):
    return jax.shard_map(
        body,
        mesh=mesh,
        in_specs=(
            P("scalp", None),
            P(("scalp", "screen"), None),
            P(("scalp", "screen"), None, None),
            P(("scalp", "screen"), None, None),
            P(("scalp", "screen"), None),
            P(("scalp", "screen"), None),
            P(("scalp", "screen"), None),
            P("screen", None, None),
            P("screen", None, None),
        ),
        out_specs=P(("scalp", "screen"), None),
        check_vma=False,
    )
```
